128 devices in a mesh: wide: 16 (over x_hi, y, core), narrow: 4 (over z), depth: 2 (over x_lo).
Axes of the slice: x: 4 (x_hi: 2, x_lo: 2; x = x_hi * 2 + x_lo), y: 4, z: 4, core: 2. Of those that a mesh axis runs over, the one named last changes fastest.
Arguments:
- hidden_state: bfloat16 [64, 4096], P(('wide', 'depth')), may hold values from -6 to 6
- query_weight: bfloat16 [4096, 4096], P('depth', 'narrow'), may hold values from -0.09375 to 0.09375
- output_weight: bfloat16 [4096, 4096], P('narrow'), may hold values from -0.09375 to 0.09375
- cache_keys: bfloat16 [64, 512, 4096], P(('wide', 'depth'), None, 'narrow'), may hold values from -128 to 128
- cache_values: bfloat16 [64, 512, 4096], P(('wide', 'depth'), None, 'narrow'), may hold values from -12 to 12
- enc_blocks: int32 [64], replicated, may hold values from 1 to 4
- cache_slot: int32 [64], replicated, may hold values from 0 to 63, as said below
Outputs:
- attended: bfloat16 [64, 4096], P(('wide', 'depth'), 'narrow')
The draws below stay inside these ranges and needn't reach their ends.
Inputs may be any that keep to these rules, and one draw needn't show every extreme that they name: Request r attends to the first 128 * enc_blocks[r] rows of its cache slot. Every slot holds exactly one request, and r and cache_slot[r] agree in their value of (index // 2) % 2.
All inputs are finite; a program needn't handle non-finite values.
Results may differ from the reference program's by a relative error of at most 0.012.
The reference program's roundings to bfloat16 on the way (of `normed`, `queries`, `shares` and `context`) count: a program that leaves them out, or rounds other values in their place, can miss the bound.
Values may be sent and summed in bfloat16 or wider, within the bound.
A program may use at most 64 MiB of HBM per device.

```python
import jax
import jax.numpy as jnp
from jax import lax

D = 4096
HEADS = 64
HDIM = 64
REQ_DEV = 2
LMAX = 512
BLOCK = 128
BLOCKS = 4
OWNERS = 16
HALVES = 2
REQUESTS = 64


def draw_cache_keys(key, part):
    arr_shape = (REQUESTS, LMAX, HEADS * HDIM)
    key_base = jax.random.fold_in(key, 0)
    return jnp.clip(jax.random.normal(key_base, arr_shape, jnp.float32) * 0.3, -2.0, 2.0).astype(jnp.bfloat16)


def draw_cache_slot(key, part):
    combos = OWNERS * REQ_DEV
    subkeys = jax.random.split(jax.random.fold_in(key, 7), HALVES)
    orders = jax.vmap(lambda subkey: jax.random.permutation(subkey, combos))(subkeys)
    request = jnp.arange(REQUESTS, dtype=jnp.int32)
    depth_of = request // REQ_DEV % HALVES
    combo_at = request // (REQ_DEV * HALVES) * REQ_DEV + request % REQ_DEV
    target = orders[depth_of, combo_at].astype(jnp.int32)
    return ((target // REQ_DEV * HALVES + depth_of) * REQ_DEV + target % REQ_DEV).astype(jnp.int32)


def touch_ends(entries, rng, least, top_value):
    longest = entries.shape.index(max(entries.shape))
    spots = []
    for shift in (0, 1):
        where = [jax.random.randint(jax.random.fold_in(rng, axis), (), 0, length) for axis, length in enumerate(entries.shape)]
        where[longest] = (where[longest] + shift) % entries.shape[longest]
        spots.append(tuple(where))
    return entries.at[spots[0]].set(least).at[spots[1]].set(top_value)


def level_of(stream_key, shape, cuts, least, high):
    factor_of, own = 1.0, jax.random.fold_in(stream_key, 6)
    for dim, shards_of in cuts:
        heights = jnp.exp(jax.random.uniform(jax.random.fold_in(own, dim), (shards_of,), jnp.float32, least / len(cuts), high / len(cuts)))
        factor_of = factor_of * jnp.repeat(heights, shape[dim] // shards_of).reshape([-1 if axis == dim else 1 for axis in range(len(shape))])
    return factor_of


def scatter_about(own_key, dims, deviation, most, cuts=(), kind=jnp.bfloat16):
    entries = jax.random.normal(own_key, dims, jnp.float32) * deviation
    if len(cuts) > 0:
        entries = level_of(own_key, dims, cuts, -0.22, 0.18) * entries
    return jnp.clip(entries, min=-most, max=most).astype(kind)


def setup_inputs(seed: int = 0) -> dict:
    key_list = jax.random.split(jax.random.key(seed), 8)
    hidden_state = scatter_about(key_list[0], (REQUESTS, D), 1.0, 6.0, ((0, 32),))
    query_weight = scatter_about(key_list[1], (D, HEADS * HDIM), D ** -0.5, 0.09375, ((0, 2), (1, 4)))
    output_weight = scatter_about(key_list[2], (HEADS * HDIM, D), (HEADS * HDIM) ** -0.5, 0.09375, ((0, 4),))
    cache_keys = draw_cache_keys(jax.random.fold_in(key_list[7], 71), 0)
    cache_values = scatter_about(key_list[4], (REQUESTS, LMAX, HEADS * HDIM), 2.0, 12.0, ((0, 32), (2, 4)))
    enc_blocks = touch_ends(jax.random.randint(key_list[5], (REQUESTS,), 1, BLOCKS + 1), jax.random.fold_in(key_list[5], 1), 1, BLOCKS).astype(jnp.int32)
    cache_slot = draw_cache_slot(jax.random.fold_in(key_list[7], 71), 0)
    return dict(hidden_state=hidden_state, query_weight=query_weight, output_weight=output_weight, cache_keys=cache_keys, cache_values=cache_values, enc_blocks=enc_blocks, cache_slot=cache_slot)


def attend_one(packed, cache_keys, cache_values, positions):
    query_row, slot_row, block_count = packed
    key_rows = lax.dynamic_index_in_dim(cache_keys, slot_row.astype(jnp.int32), 0, keepdims=False)
    value_rows = lax.dynamic_index_in_dim(cache_values, slot_row.astype(jnp.int32), 0, keepdims=False)
    query_heads = query_row.reshape(HEADS, HDIM).astype(jnp.float32)
    key_heads = key_rows.reshape(LMAX, HEADS, HDIM).astype(jnp.float32)
    value_heads = value_rows.reshape(LMAX, HEADS, HDIM).astype(jnp.float32)
    scores = jnp.einsum('hd,lhd->hl', query_heads, key_heads)
    usable = positions < block_count.astype(jnp.int32) * BLOCK
    scores = jnp.where(usable[None, :], scores, jnp.float32(-1e+30))
    row_top = lax.optimization_barrier(jnp.max(scores, axis=-1, keepdims=True))
    raised = jnp.exp(scores - row_top)
    shares = (raised / lax.optimization_barrier(jnp.sum(raised, axis=-1, keepdims=True))).astype(jnp.bfloat16)
    context = jnp.einsum('hl,lhd->hd', shares.astype(jnp.float32), value_heads)
    return context.reshape(HEADS * HDIM).astype(jnp.bfloat16)

def reference(hidden_state, query_weight, output_weight, cache_keys, cache_values, enc_blocks, cache_slot):
    widened = hidden_state.astype(jnp.float32)
    mean_square = lax.optimization_barrier(jnp.mean(widened * widened, axis=-1, keepdims=True))
    normed = (widened * lax.rsqrt(mean_square + 1e-06)).astype(jnp.bfloat16)
    queries = jnp.dot(normed, query_weight, preferred_element_type=jnp.float32).astype(jnp.bfloat16)
    positions = jnp.arange(LMAX, dtype=jnp.int32)
    context = lax.map(lambda packed: attend_one(packed, cache_keys, cache_values, positions), (queries, cache_slot, enc_blocks))
    return jnp.dot(context, output_weight, preferred_element_type=jnp.float32).astype(jnp.bfloat16)
```

```python
import jax
import jax.numpy as jnp
from jax import lax
from jax.experimental import pallas as pl
from jax.experimental.pallas import tpu as pltpu
from jax.sharding import PartitionSpec as P

HDIM = 64
BLOCK = 128
XH, Y, C = 2, 4, 2
WIDE, NARROW, DEPTH = 16, 4, 2
ROWS = 2
MESH = pl.DeviceIdType.MESH


def kernel(
    hid, wq, wo, keys, vals, enc_blocks, cache_slot, out,
    hid_v, wq_v, wo_v, k_v, v_v,
    norm_own, norm_got, part_out, part_got, q_own, q_all, ctx_v,
    out_part, out_got, fin_all,
    ld_sem, a_send, a_recv, x_send, x_recv, y_send, y_recv, e_send, e_recv, f_send, f_recv,
):
    w = lax.axis_index("wide")
    z = lax.axis_index("narrow")
    d = lax.axis_index("depth")
    xh, y, c = w // 8, (w // 2) % 4, w % 2
    half = wq.shape[0]
    feats = wq.shape[1]
    heads = feats // HDIM

    def wide_of(xh_, y_, c_):
        return xh_ * 8 + y_ * 2 + c_

    def peer(w_, z_, d_):
        return {"wide": w_, "narrow": z_, "depth": d_}

    def remote(src, dst, send, recv, to):
        return pltpu.make_async_remote_copy(
            src_ref=src, dst_ref=dst, send_sem=send, recv_sem=recv, device_id=to, device_id_type=MESH
        )

    ld_hid = pltpu.make_async_copy(hid, hid_v, ld_sem.at[0])
    ld_wq = pltpu.make_async_copy(wq, wq_v, ld_sem.at[1])
    ld_k = pltpu.make_async_copy(keys, k_v, ld_sem.at[2])
    ld_v = pltpu.make_async_copy(vals, v_v, ld_sem.at[3])
    ld_wo = [
        pltpu.make_async_copy(
            wo.at[:, pl.ds(pl.multiple_of((z + dz) % 4 * feats, feats), feats)], wo_v.at[dz], ld_sem.at[4 + dz]
        )
        for dz in range(4)
    ]
    ld_hid.start()
    ld_wq.start()
    ld_k.start()
    ld_v.start()
    for dz in (2, 1, 3, 0):
        ld_wo[dz].start()

    barrier = pltpu.get_barrier_semaphore()
    peers = [peer((w + o) % WIDE, z, d) for o in range(1, WIDE)]
    peers += [peer(w, z, 1 - d), peer(wide_of(1 - xh, y, c), z, 1 - d)]
    peers += [peer(w, (z + o) % NARROW, d) for o in range(1, NARROW)]
    for p in peers:
        pl.semaphore_signal(barrier, inc=1, device_id=p, device_id_type=MESH)

    ld_hid.wait()
    wide_hid = hid_v[...].astype(jnp.float32)
    mean_square = jnp.mean(wide_hid * wide_hid, axis=-1, keepdims=True)
    normed = (wide_hid * lax.rsqrt(mean_square + 1e-06)).astype(jnp.bfloat16)
    norm_own[0] = normed[:, :half]
    norm_own[1] = normed[:, half:]

    slot_req = []
    for i in range(ROWS):
        mine = (w * DEPTH + d) * ROWS + i
        req = jnp.int32(0)
        for j in range(WIDE * ROWS):
            cand = (j // ROWS * DEPTH + d) * ROWS + j % ROWS
            req = jnp.where(cache_slot[cand] == mine, cand, req)
        slot_req.append(req)

    pl.semaphore_wait(barrier, len(peers))

    cp_a = remote(norm_own.at[1 - d], norm_got, a_send, a_recv, peer(w, z, 1 - d))
    cp_a.start()
    ld_wq.wait()
    cp_a.wait_recv()
    lhs = jnp.concatenate(
        [norm_own[d].astype(jnp.float32), norm_got[...].astype(jnp.float32)], axis=0
    ).astype(jnp.bfloat16)
    part = jnp.dot(lhs, wq_v[...], preferred_element_type=jnp.float32)
    part_out[0] = part[:ROWS]
    part_out[1] = part[ROWS:]
    other_w = wide_of(1 - xh, y, c)
    cp_x = [
        remote(part_out.at[0], part_got.at[0], x_send.at[0], x_recv.at[0], peer(other_w, z, d)),
        remote(part_out.at[1], part_got.at[1], x_send.at[1], x_recv.at[1], peer(w, z, 1 - d)),
        remote(part_out.at[1], part_got.at[2], x_send.at[2], x_recv.at[2], peer(other_w, z, 1 - d)),
    ]
    for cp in cp_x:
        cp.start()
    for cp in cp_x:
        cp.wait_recv()
    q_own[xh] = (part_out[0] + part_got[1]).astype(jnp.bfloat16)
    q_own[1 - xh] = (part_got[0] + part_got[2]).astype(jnp.bfloat16)

    yc = y * 2 + c
    cp_y = []
    for o in range(1, Y * C):
        yc_to = (yc + o) % (Y * C)
        cp_y.append(
            remote(q_own, q_all.at[yc], y_send.at[o], y_recv.at[o], peer(xh * 8 + yc_to, z, d))
        )
    for cp in cp_y:
        cp.start()
    q_all[yc] = q_own[...]
    ld_k.wait()
    ld_v.wait()
    for o in range(1, Y * C):
        yc_from = (yc + Y * C - o) % (Y * C)
        remote(q_own, q_all.at[yc_from], y_send.at[o], y_recv.at[o], peer(w, z, d)).wait_recv()

    head_of = lax.broadcasted_iota(jnp.int32, (heads, feats), 1) // HDIM
    own_head = head_of == lax.broadcasted_iota(jnp.int32, (heads, feats), 0)
    row_id = lax.broadcasted_iota(jnp.int32, (ROWS, feats), 0)
    for i in range(ROWS):
        req = slot_req[i]
        src = req // (DEPTH * ROWS)
        pair = q_all[src % 8, src // 8].astype(jnp.float32)
        query = jnp.sum(jnp.where(row_id == req % ROWS, pair, 0.0), axis=0, keepdims=True)
        spread = jnp.where(own_head, query, 0.0).astype(jnp.bfloat16)
        scores = lax.dot_general(
            spread, k_v[i], (((1,), (1,)), ((), ())), preferred_element_type=jnp.float32
        )
        position = lax.broadcasted_iota(jnp.int32, scores.shape, 1)
        scores = jnp.where(position < enc_blocks[req] * BLOCK, scores, -1e30)
        raised = jnp.exp(scores - jnp.max(scores, axis=-1, keepdims=True))
        shares = (raised / jnp.sum(raised, axis=-1, keepdims=True)).astype(jnp.bfloat16)
        ctx = jnp.dot(shares, v_v[i], preferred_element_type=jnp.float32)
        ctx = jnp.sum(jnp.where(own_head, ctx, 0.0), axis=0, keepdims=True)
        ctx_v[pl.ds(i, 1), :] = ctx

    ctx_b = ctx_v[...].astype(jnp.bfloat16)
    cp_e = {}
    for dz in (2, 1, 3):
        ld_wo[dz].wait()
        out_part[dz] = jnp.dot(ctx_b, wo_v[dz], preferred_element_type=jnp.float32)
        cp_e[dz] = remote(
            out_part.at[dz], out_got.at[dz], e_send.at[dz], e_recv.at[dz], peer(w, (z + dz) % NARROW, d)
        )
        cp_e[dz].start()
    ld_wo[0].wait()
    total = jnp.dot(ctx_b, wo_v[0], preferred_element_type=jnp.float32)
    for dz in (1, 3, 2):
        cp_e[dz].wait_recv()
        total = total + out_got[dz]
    fin_all[w] = total.astype(jnp.bfloat16)

    cp_f = []
    for o in range(1, WIDE):
        cp_f.append(
            remote(fin_all.at[w], fin_all.at[w], f_send.at[o], f_recv.at[o], peer((w + o) % WIDE, z, d))
        )
    for cp in cp_f:
        cp.start()
    for o in range(1, WIDE):
        src = (w + WIDE - o) % WIDE
        remote(fin_all.at[src], fin_all.at[src], f_send.at[o], f_recv.at[o], peer(w, z, d)).wait_recv()
    rows = []
    for i in range(ROWS):
        slot = cache_slot[(w * DEPTH + d) * ROWS + i]
        pair = fin_all[slot // (DEPTH * ROWS)].astype(jnp.float32)
        rows.append(jnp.sum(jnp.where(row_id == slot % ROWS, pair, 0.0), axis=0, keepdims=True))
    out[...] = jnp.concatenate(rows, axis=0).astype(jnp.bfloat16)

    cp_a.wait_send()
    for cp in cp_x + cp_y + list(cp_e.values()) + cp_f:
        cp.wait_send()


def shards(hidden_state, query_weight, output_weight, cache_keys, cache_values, enc_blocks, cache_slot):
    rows, width = hidden_state.shape
    half, feats = query_weight.shape
    bf16, f32 = jnp.bfloat16, jnp.float32
    dma = pltpu.SemaphoreType.DMA
    any_spec = pl.BlockSpec(memory_space=pl.ANY)
    smem = pl.BlockSpec(memory_space=pltpu.SMEM)
    return pl.pallas_call(
        kernel,
        out_shape=jax.ShapeDtypeStruct((rows, feats), bf16),
        in_specs=[any_spec] * 5 + [smem] * 2,
        out_specs=pl.BlockSpec(memory_space=pltpu.VMEM),
        scratch_shapes=[
            pltpu.VMEM((rows, width), bf16),
            pltpu.VMEM((half, feats), bf16),
            pltpu.VMEM((NARROW, feats, feats), bf16),
            pltpu.VMEM(cache_keys.shape, bf16),
            pltpu.VMEM(cache_values.shape, bf16),
            pltpu.VMEM((2, rows, half), bf16),
            pltpu.VMEM((rows, half), bf16),
            pltpu.VMEM((2, rows, feats), f32),
            pltpu.VMEM((3, rows, feats), f32),
            pltpu.VMEM((XH, rows, feats), bf16),
            pltpu.VMEM((Y * C, XH, rows, feats), bf16),
            pltpu.VMEM((rows, feats), f32),
            pltpu.VMEM((NARROW, rows, feats), f32),
            pltpu.VMEM((NARROW, rows, feats), f32),
            pltpu.VMEM((WIDE, rows, feats), bf16),
            dma((8,)), dma, dma, dma((3,)), dma((3,)), dma((8,)), dma((8,)),
            dma((4,)), dma((4,)), dma((16,)), dma((16,)),
        ],
        compiler_params=pltpu.CompilerParams(
            collective_id=0, has_side_effects=True, vmem_limit_bytes=48 * 1024 * 1024
        ),
    )(hidden_state, query_weight, output_weight, cache_keys, cache_values, enc_blocks, cache_slot)


def solution(mesh):
    placed = (
        P(("wide", "depth"), None),
        P("depth", "narrow"),
        P("narrow", None),
        P(("wide", "depth"), None, "narrow"),
        P(("wide", "depth"), None, "narrow"),
        P(),
        P(),
    )
    return jax.shard_map(
        shards,
        mesh=mesh,
        in_specs=placed,
        out_specs=P(("wide", "depth"), "narrow"),
        check_vma=False,
    )
```

```python
import jax
import jax.numpy as jnp
from jax import lax
from jax.experimental import pallas as pl
from jax.experimental.pallas import tpu as pltpu
from jax.sharding import PartitionSpec as P

HDIM = 64
BLOCK = 128
XH, Y, C = 2, 4, 2
WIDE, NARROW, DEPTH = 16, 4, 2
ROWS = 2
MESH = pl.DeviceIdType.MESH
FAR = (2, 1, 3, 0)
STEPS = [(a, b, e) for a in (1, 0) for b in FAR for e in (0, 1)]


def kernel(
    hid, wq, wo, keys, vals, enc_hbm, slot_hbm, out,
    hid_v, wq_v, wo_v, k_v, v_v, enc_blocks, cache_slot,
    norm_own, norm_got, q_own, q_out, q_oth, ctx_v,
    out_part, out_got, fin_all,
    ld_sem, a_send, a_recv, p_send, p_recv, o_send, o_recv, e_send, e_recv, f_send, f_recv,
):
    w = lax.axis_index("wide")
    z = lax.axis_index("narrow")
    d = lax.axis_index("depth")
    xh, y, c = w // 8, (w // 2) % 4, w % 2
    half = wq.shape[0]
    feats = wq.shape[1]
    heads = feats // HDIM

    def wide_at(step, sign):
        return (xh + step[0]) % XH * 8 + (y + sign * step[1] + Y) % Y * 2 + (c + step[2]) % C

    def peer(w_, z_, d_):
        return {"wide": w_, "narrow": z_, "depth": d_}

    def remote(src, dst, send, recv, to):
        return pltpu.make_async_remote_copy(
            src_ref=src, dst_ref=dst, send_sem=send, recv_sem=recv, device_id=to, device_id_type=MESH
        )

    barrier = pltpu.get_barrier_semaphore()
    peers = [peer(wide_at(s, 1), z, d) for s in STEPS if s != (0, 0, 0)]
    peers += [peer(wide_at(s, 1), z, 1 - d) for s in STEPS]
    peers += [peer(w, (z + o) % NARROW, d) for o in range(1, NARROW)]
    for p in peers:
        pl.semaphore_signal(barrier, inc=1, device_id=p, device_id_type=MESH)

    ld_hid = pltpu.make_async_copy(hid, hid_v, ld_sem.at[0])
    ld_wq = pltpu.make_async_copy(wq, wq_v, ld_sem.at[1])
    ld_k = pltpu.make_async_copy(keys, k_v, ld_sem.at[2])
    ld_v = pltpu.make_async_copy(vals, v_v, ld_sem.at[3])
    ld_wo = [
        pltpu.make_async_copy(
            wo.at[:, pl.ds(pl.multiple_of((z + dz) % 4 * feats, feats), feats)], wo_v.at[dz], ld_sem.at[4 + dz]
        )
        for dz in range(4)
    ]
    ld_enc = pltpu.make_async_copy(enc_hbm, enc_blocks, ld_sem.at[8])
    ld_slot = pltpu.make_async_copy(slot_hbm, cache_slot, ld_sem.at[9])
    ld_hid.start()
    ld_enc.start()
    ld_slot.start()
    ld_wq.start()
    ld_k.start()
    ld_v.start()
    for dz in (2, 1, 3, 0):
        ld_wo[dz].start()

    ld_hid.wait()
    wide_hid = hid_v[...].astype(jnp.float32)
    mean_square = jnp.mean(wide_hid * wide_hid, axis=-1, keepdims=True)
    normed = (wide_hid * lax.rsqrt(mean_square + 1e-06)).astype(jnp.bfloat16)
    norm_own[0] = normed[:, :half]
    norm_own[1] = normed[:, half:]

    ld_enc.wait()
    ld_slot.wait()
    slot_req = []
    for i in range(ROWS):
        mine = (w * DEPTH + d) * ROWS + i
        req = jnp.int32(0)
        for j in range(WIDE * ROWS):
            cand = (j // ROWS * DEPTH + d) * ROWS + j % ROWS
            req = jnp.where(cache_slot[cand] == mine, cand, req)
        slot_req.append(req)

    pl.semaphore_wait(barrier, len(peers))
    cp_a = remote(norm_own.at[1 - d], norm_got, a_send, a_recv, peer(w, z, 1 - d))
    cp_a.start()

    ld_wq.wait()
    q_own[w] = jnp.dot(norm_own[d], wq_v[...], preferred_element_type=jnp.float32)
    cp_p = [
        remote(q_own.at[w], q_own.at[w], p_send.at[i], p_recv.at[i], peer(wide_at(s, 1), z, d))
        for i, s in enumerate(STEPS[:-2] + STEPS[-1:])
    ]
    for cp in cp_p:
        cp.start()

    cp_a.wait_recv()
    q_out[...] = jnp.dot(norm_got[...], wq_v[...], preferred_element_type=jnp.float32)
    cp_o = [
        remote(q_out, q_oth.at[w], o_send.at[i], o_recv.at[i], peer(wide_at(s, 1), z, 1 - d))
        for i, s in enumerate(STEPS)
    ]
    for cp in cp_o:
        cp.start()

    ld_k.wait()
    ld_v.wait()
    for i, s in enumerate(STEPS[:-2] + STEPS[-1:]):
        src = wide_at(s, -1)
        remote(q_own.at[src], q_own.at[src], p_send.at[i], p_recv.at[i], peer(w, z, 1 - d)).wait_recv()
    for i, s in enumerate(STEPS):
        src = wide_at(s, -1)
        remote(q_out, q_oth.at[src], o_send.at[i], o_recv.at[i], peer(w, z, 1 - d)).wait_recv()
    head_of = lax.broadcasted_iota(jnp.int32, (heads, feats), 1) // HDIM
    own_head = head_of == lax.broadcasted_iota(jnp.int32, (heads, feats), 0)
    row_id = lax.broadcasted_iota(jnp.int32, (ROWS, feats), 0)
    for i in range(ROWS):
        req = slot_req[i]
        src = req // (DEPTH * ROWS)
        pair = (q_own[src] + q_oth[src]).astype(jnp.bfloat16).astype(jnp.float32)
        query = jnp.sum(jnp.where(row_id == req % ROWS, pair, 0.0), axis=0, keepdims=True)
        spread = jnp.where(own_head, query, 0.0).astype(jnp.bfloat16)
        scores = lax.dot_general(
            spread, k_v[i], (((1,), (1,)), ((), ())), preferred_element_type=jnp.float32
        )
        position = lax.broadcasted_iota(jnp.int32, scores.shape, 1)
        scores = jnp.where(position < enc_blocks[req] * BLOCK, scores, -1e30)
        raised = jnp.exp(scores - jnp.max(scores, axis=-1, keepdims=True))
        shares = (raised / jnp.sum(raised, axis=-1, keepdims=True)).astype(jnp.bfloat16)
        ctx = jnp.dot(shares, v_v[i], preferred_element_type=jnp.float32)
        ctx = jnp.sum(jnp.where(own_head, ctx, 0.0), axis=0, keepdims=True)
        ctx_v[pl.ds(i, 1), :] = ctx
    ctx_b = ctx_v[...].astype(jnp.bfloat16)
    cp_e = {}
    for dz in (2, 1, 3):
        ld_wo[dz].wait()
        out_part[dz] = jnp.dot(ctx_b, wo_v[dz], preferred_element_type=jnp.float32)
        cp_e[dz] = remote(
            out_part.at[dz], out_got.at[dz], e_send.at[dz], e_recv.at[dz], peer(w, (z + dz) % NARROW, d)
        )
        cp_e[dz].start()
    ld_wo[0].wait()
    total = jnp.dot(ctx_b, wo_v[0], preferred_element_type=jnp.float32)
    for dz in (1, 3, 2):
        cp_e[dz].wait_recv()
        total = total + out_got[dz]
    fin_all[w] = total.astype(jnp.bfloat16)
    cp_f = []
    for i, s in enumerate(STEPS[:-2] + STEPS[-1:]):
        cp_f.append(
            remote(fin_all.at[w], fin_all.at[w], f_send.at[i], f_recv.at[i], peer(wide_at(s, 1), z, d))
        )
    for cp in cp_f:
        cp.start()
    for i, s in enumerate(STEPS[:-2] + STEPS[-1:]):
        src = wide_at(s, -1)
        remote(fin_all.at[src], fin_all.at[src], f_send.at[i], f_recv.at[i], peer(w, z, 1 - d)).wait_recv()
    rows = []
    for i in range(ROWS):
        slot = cache_slot[(w * DEPTH + d) * ROWS + i]
        pair = fin_all[slot // (DEPTH * ROWS)].astype(jnp.float32)
        rows.append(jnp.sum(jnp.where(row_id == slot % ROWS, pair, 0.0), axis=0, keepdims=True))
    out[...] = jnp.concatenate(rows, axis=0).astype(jnp.bfloat16)

    for cp in [cp_a] + cp_p + cp_o + list(cp_e.values()) + cp_f:
        cp.wait_send()


def shards(hidden_state, query_weight, output_weight, cache_keys, cache_values, enc_blocks, cache_slot):
    rows, width = hidden_state.shape
    half, feats = query_weight.shape
    bf16, f32 = jnp.bfloat16, jnp.float32
    dma = pltpu.SemaphoreType.DMA
    any_spec = pl.BlockSpec(memory_space=pl.ANY)
    return pl.pallas_call(
        kernel,
        out_shape=jax.ShapeDtypeStruct((rows, feats), bf16),
        in_specs=[any_spec] * 7,
        out_specs=pl.BlockSpec(memory_space=pltpu.VMEM),
        scratch_shapes=[
            pltpu.VMEM((rows, width), bf16),
            pltpu.VMEM((half, feats), bf16),
            pltpu.VMEM((NARROW, feats, feats), bf16),
            pltpu.VMEM(cache_keys.shape, bf16),
            pltpu.VMEM(cache_values.shape, bf16),
            pltpu.SMEM(enc_blocks.shape, jnp.int32),
            pltpu.SMEM(cache_slot.shape, jnp.int32),
            pltpu.VMEM((2, rows, half), bf16),
            pltpu.VMEM((rows, half), bf16),
            pltpu.VMEM((WIDE, rows, feats), f32),
            pltpu.VMEM((rows, feats), f32),
            pltpu.VMEM((WIDE, rows, feats), f32),
            pltpu.VMEM((rows, feats), f32),
            pltpu.VMEM((NARROW, rows, feats), f32),
            pltpu.VMEM((NARROW, rows, feats), f32),
            pltpu.VMEM((WIDE, rows, feats), bf16),
            dma((10,)), dma, dma, dma((15,)), dma((15,)), dma((16,)), dma((16,)),
            dma((4,)), dma((4,)), dma((15,)), dma((15,)),
        ],
        compiler_params=pltpu.CompilerParams(
            collective_id=0, has_side_effects=True, vmem_limit_bytes=67_043_328
        ),
    )(hidden_state, query_weight, output_weight, cache_keys, cache_values, enc_blocks, cache_slot)


def solution(mesh):
    placed = (
        P(("wide", "depth"), None),
        P("depth", "narrow"),
        P("narrow", None),
        P(("wide", "depth"), None, "narrow"),
        P(("wide", "depth"), None, "narrow"),
        P(),
        P(),
    )
    return jax.shard_map(
        shards,
        mesh=mesh,
        in_specs=placed,
        out_specs=P(("wide", "depth"), "narrow"),
        check_vma=False,
    )
```

```python
import jax
import jax.numpy as jnp
from jax import lax
from jax.experimental import pallas as pl
from jax.experimental.pallas import tpu as pltpu
from jax.sharding import PartitionSpec as P

HDIM = 64
BLOCK = 128
XH, Y, C = 2, 4, 2
WIDE, NARROW, DEPTH = 16, 4, 2
ROWS = 2
MESH = pl.DeviceIdType.MESH
FAR = (2, 1, 3, 0)
STEPS = [(a, b, e) for a in (1, 0) for b in FAR for e in (0, 1)]


def kernel(
    hid, wq, wo, keys, vals, enc_hbm, slot_hbm, out,
    hid_v, wq_v, wo_v, k_v, v_v, enc_blocks, cache_slot,
    norm_own, norm_got, q_own, q_out, q_oth, ctx_v,
    fin_out, fin_all,
    in_sem, ld_sem, a_send, a_recv, p_send, p_recv, o_send, o_recv, e_send, e_recv,
):
    w = lax.axis_index("wide")
    z = lax.axis_index("narrow")
    d = lax.axis_index("depth")
    xh, y, c = w // 8, (w // 2) % 4, w % 2
    half = wq.shape[0]
    feats = wq.shape[1]
    heads = feats // HDIM

    def wide_at(step, sign):
        return (xh + step[0]) % XH * 8 + (y + sign * step[1] + Y) % Y * 2 + (c + step[2]) % C

    def peer(w_, z_, d_):
        return {"wide": w_, "narrow": z_, "depth": d_}

    def remote(src, dst, send, recv, to):
        return pltpu.make_async_remote_copy(
            src_ref=src, dst_ref=dst, send_sem=send, recv_sem=recv, device_id=to, device_id_type=MESH
        )

    barrier = pltpu.get_barrier_semaphore()
    peers = [peer(wide_at(s, 1), z, d) for s in STEPS if s != (0, 0, 0)]
    peers += [peer(wide_at(s, 1), z, 1 - d) for s in STEPS]
    peers += [peer(w, (z + o) % NARROW, d) for o in range(1, NARROW)]
    for p in peers:
        pl.semaphore_signal(barrier, inc=1, device_id=p, device_id_type=MESH)

    ld_hid = pltpu.make_async_copy(hid, hid_v, ld_sem.at[0])
    ld_wq = pltpu.make_async_copy(wq, wq_v, ld_sem.at[1])
    ld_k = pltpu.make_async_copy(keys, k_v, ld_sem.at[2])
    ld_v = pltpu.make_async_copy(vals, v_v, ld_sem.at[3])
    ld_wo = [
        pltpu.make_async_copy(
            wo.at[:, pl.ds(pl.multiple_of((z + dz) % 4 * feats, feats), feats)], wo_v.at[dz], ld_sem.at[4 + dz]
        )
        for dz in range(4)
    ]
    ld_enc = pltpu.make_async_copy(enc_hbm, enc_blocks, ld_sem.at[8])
    ld_slot = pltpu.make_async_copy(slot_hbm, cache_slot, ld_sem.at[9])
    ld_hid.start()
    ld_enc.start()
    ld_slot.start()
    ld_wq.start()
    ld_k.start()
    ld_v.start()
    for dz in (2, 1, 3, 0):
        ld_wo[dz].start()

    ld_hid.wait()
    wide_hid = hid_v[...].astype(jnp.float32)
    mean_square = jnp.mean(wide_hid * wide_hid, axis=-1, keepdims=True)
    normed = (wide_hid * lax.rsqrt(mean_square + 1e-06)).astype(jnp.bfloat16)
    norm_own[0] = normed[:, :half]
    norm_own[1] = normed[:, half:]

    ld_enc.wait()
    ld_slot.wait()
    slot_req = []
    for i in range(ROWS):
        mine = (w * DEPTH + d) * ROWS + i
        req = jnp.int32(0)
        for j in range(WIDE * ROWS):
            cand = (j // ROWS * DEPTH + d) * ROWS + j % ROWS
            req = jnp.where(cache_slot[cand] == mine, cand, req)
        slot_req.append(req)

    pl.semaphore_wait(barrier, len(peers))
    cp_a = remote(norm_own.at[1 - d], norm_got, a_send, a_recv, peer(w, z, 1 - d))
    cp_a.start()
    for o in range(1, NARROW):
        pl.semaphore_signal(in_sem, inc=1, device_id=peer(w, (z + o) % NARROW, d), device_id_type=MESH)

    ld_wq.wait()
    q_own[w] = jnp.dot(norm_own[d], wq_v[...], preferred_element_type=jnp.float32)
    cp_p = [
        remote(q_own.at[w], q_own.at[w], p_send.at[i], p_recv.at[i], peer(wide_at(s, 1), z, d))
        for i, s in enumerate(STEPS[:-2] + STEPS[-1:])
    ]
    for cp in cp_p:
        cp.start()

    cp_a.wait_recv()
    q_out[...] = jnp.dot(norm_got[...], wq_v[...], preferred_element_type=jnp.float32)
    cp_o = [
        remote(q_out, q_oth.at[w], o_send.at[i], o_recv.at[i], peer(wide_at(s, 1), z, 1 - d))
        for i, s in enumerate(STEPS)
    ]
    for cp in cp_o:
        cp.start()

    ld_k.wait()
    ld_v.wait()
    for i, s in enumerate(STEPS[:-2] + STEPS[-1:]):
        src = wide_at(s, -1)
        remote(q_own.at[src], q_own.at[src], p_send.at[i], p_recv.at[i], peer(w, z, 1 - d)).wait_recv()
    for i, s in enumerate(STEPS):
        src = wide_at(s, -1)
        remote(q_out, q_oth.at[src], o_send.at[i], o_recv.at[i], peer(w, z, 1 - d)).wait_recv()
    head_of = lax.broadcasted_iota(jnp.int32, (heads, feats), 1) // HDIM
    own_head = head_of == lax.broadcasted_iota(jnp.int32, (heads, feats), 0)
    row_id = lax.broadcasted_iota(jnp.int32, (ROWS, feats), 0)
    scores = []
    for i in range(ROWS):
        req = slot_req[i]
        src = req // (DEPTH * ROWS)
        pair = (q_own[src] + q_oth[src]).astype(jnp.bfloat16).astype(jnp.float32)
        query = jnp.sum(jnp.where(row_id == req % ROWS, pair, 0.0), axis=0, keepdims=True)
        spread = jnp.where(own_head, query, 0.0).astype(jnp.bfloat16)
        score = lax.dot_general(
            spread, k_v[i], (((1,), (1,)), ((), ())), preferred_element_type=jnp.float32
        )
        position = lax.broadcasted_iota(jnp.int32, score.shape, 1)
        scores.append(jnp.where(position < enc_blocks[req] * BLOCK, score, -1e30))
    scores = jnp.concatenate(scores, axis=0)
    raised = jnp.exp(scores - jnp.max(scores, axis=-1, keepdims=True))
    shares = (raised / jnp.sum(raised, axis=-1, keepdims=True)).astype(jnp.bfloat16)
    for i in range(ROWS):
        ctx = jnp.dot(shares[i * heads : (i + 1) * heads], v_v[i], preferred_element_type=jnp.float32)
        ctx_v[pl.ds(i, 1), :] = jnp.sum(jnp.where(own_head, ctx, 0.0), axis=0, keepdims=True)
    ctx_b = ctx_v[...].astype(jnp.bfloat16)
    cp_e = []
    from_e = []
    for dz in (2, 1, 3, 0):
        ld_wo[dz].wait()
        block = jnp.dot(ctx_b, wo_v[dz], preferred_element_type=jnp.float32).astype(jnp.bfloat16)
        fin_out[dz] = block
        if dz == 0:
            fin_all[0, w] = block
        if dz == 2:
            pl.semaphore_wait(in_sem, NARROW - 1)
        for s in STEPS:
            if s == (0, 0, 0) and dz == 0:
                continue
            i = dz * WIDE + STEPS.index(s)
            to, src = wide_at(s, 1), wide_at(s, -1)
            cp_e.append(
                remote(fin_out.at[dz], fin_all.at[dz, w], e_send.at[i], e_recv.at[i], peer(to, (z + dz) % NARROW, d))
            )
            from_e.append(
                remote(fin_out.at[dz], fin_all.at[dz, src], e_send.at[i], e_recv.at[i], peer(w, z, 1 - d))
            )
            cp_e[-1].start()
    for cp in from_e:
        cp.wait_recv()
    rows = []
    for i in range(ROWS):
        slot = cache_slot[(w * DEPTH + d) * ROWS + i]
        src = slot // (DEPTH * ROWS)
        pair = fin_all[0, src].astype(jnp.float32)
        for dz in range(1, NARROW):
            pair = pair + fin_all[dz, src].astype(jnp.float32)
        rows.append(jnp.sum(jnp.where(row_id == slot % ROWS, pair, 0.0), axis=0, keepdims=True))
    out[...] = jnp.concatenate(rows, axis=0).astype(jnp.bfloat16)

    for cp in [cp_a] + cp_p + cp_o + cp_e:
        cp.wait_send()


def shards(hidden_state, query_weight, output_weight, cache_keys, cache_values, enc_blocks, cache_slot):
    rows, width = hidden_state.shape
    half, feats = query_weight.shape
    bf16, f32 = jnp.bfloat16, jnp.float32
    dma = pltpu.SemaphoreType.DMA
    any_spec = pl.BlockSpec(memory_space=pltpu.HBM)
    operands = [
        pltpu.with_memory_space_constraint(a, pltpu.HBM)
        for a in (hidden_state, query_weight, output_weight, cache_keys, cache_values, enc_blocks, cache_slot)
    ]
    return pl.pallas_call(
        kernel,
        out_shape=jax.ShapeDtypeStruct((rows, feats), bf16),
        in_specs=[any_spec] * 7,
        out_specs=pl.BlockSpec(memory_space=pltpu.VMEM),
        scratch_shapes=[
            pltpu.VMEM((rows, width), bf16),
            pltpu.VMEM((half, feats), bf16),
            pltpu.VMEM((NARROW, feats, feats), bf16),
            pltpu.VMEM(cache_keys.shape, bf16),
            pltpu.VMEM(cache_values.shape, bf16),
            pltpu.SMEM(enc_blocks.shape, jnp.int32),
            pltpu.SMEM(cache_slot.shape, jnp.int32),
            pltpu.VMEM((2, rows, half), bf16),
            pltpu.VMEM((rows, half), bf16),
            pltpu.VMEM((WIDE, rows, feats), f32),
            pltpu.VMEM((rows, feats), f32),
            pltpu.VMEM((WIDE, rows, feats), f32),
            pltpu.VMEM((rows, feats), f32),
            pltpu.VMEM((NARROW, rows, feats), bf16),
            pltpu.VMEM((NARROW, WIDE, rows, feats), bf16),
            pltpu.SemaphoreType.REGULAR,
            dma((10,)), dma, dma, dma((15,)), dma((15,)), dma((16,)), dma((16,)),
            dma((64,)), dma((64,)),
        ],
        compiler_params=pltpu.CompilerParams(
            collective_id=0, has_side_effects=True, vmem_limit_bytes=48 * 1024 * 1024
        ),
    )(*operands)


def solution(mesh):
    placed = (
        P(("wide", "depth"), None),
        P("depth", "narrow"),
        P("narrow", None),
        P(("wide", "depth"), None, "narrow"),
        P(("wide", "depth"), None, "narrow"),
        P(),
        P(),
    )
    return jax.shard_map(
        shards,
        mesh=mesh,
        in_specs=placed,
        out_specs=P(("wide", "depth"), "narrow"),
        check_vma=False,
    )
```

```python
import jax
import jax.numpy as jnp
from jax import lax
from jax.experimental import pallas as pl
from jax.experimental.pallas import tpu as pltpu
from jax.sharding import PartitionSpec as P

HDIM = 64
BLOCK = 128
XH, Y, C = 2, 4, 2
WIDE, NARROW, DEPTH = 16, 4, 2
ROWS = 2
MESH = pl.DeviceIdType.MESH
STEPS = [(a, b, e) for a in (1, 0) for b in (2, 1, 3, 0) for e in (1, 0)]
HOPS = STEPS[:-1]


def kernel(
    hid, wq, wo, keys, vals, enc_hbm, slot_hbm, out,
    hid_v, wq_v, wo_v, k_v, v_v, enc_blocks, cache_slot,
    norm_own, norm_got, q_own, q_out, q_oth, ctx_v, fin_out, fin_all,
    in_sem, ld_sem, send_sem, recv_sem,
):
    w = lax.axis_index("wide")
    z = lax.axis_index("narrow")
    d = lax.axis_index("depth")
    xh, y, c = w // 8, (w // 2) % 4, w % 2
    half = wq.shape[0]
    feats = wq.shape[1]
    cols = feats // C
    heads = feats // HDIM

    def wide_at(step):
        return (xh + step[0]) % XH * 8 + (y + step[1]) % Y * 2 + (c + step[2]) % C

    def peer(w_, z_, d_):
        return {"wide": w_, "narrow": z_, "depth": d_}

    def send(src, dst, which, to):
        cp = pltpu.make_async_remote_copy(
            src_ref=src, dst_ref=dst, send_sem=send_sem.at[which], recv_sem=recv_sem.at[which],
            device_id=to, device_id_type=MESH,
        )
        cp.start()

    def wait_bytes(ref, sem):
        pltpu.make_async_copy(ref, ref, sem).wait()

    barrier = pltpu.get_barrier_semaphore()
    peers = [peer(wide_at(s), z, d) for s in HOPS]
    peers += [peer(wide_at(s), z, 1 - d) for s in STEPS]
    peers += [peer(w, (z + o) % NARROW, d) for o in (2, 1, 3)]
    for p in peers:
        pl.semaphore_signal(barrier, inc=1, device_id=p, device_id_type=MESH)

    ld_hid = pltpu.make_async_copy(hid, hid_v, ld_sem.at[0])
    ld_wq = pltpu.make_async_copy(wq, wq_v, ld_sem.at[1])
    ld_k = pltpu.make_async_copy(keys, k_v, ld_sem.at[2])
    ld_v = pltpu.make_async_copy(vals, v_v, ld_sem.at[3])
    ld_wo = [
        pltpu.make_async_copy(
            wo.at[:, pl.ds(pl.multiple_of((z + dz) % 4 * feats, feats), feats)], wo_v.at[dz], ld_sem.at[4 + dz]
        )
        for dz in range(4)
    ]
    ld_enc = pltpu.make_async_copy(enc_hbm, enc_blocks, ld_sem.at[8])
    ld_slot = pltpu.make_async_copy(slot_hbm, cache_slot, ld_sem.at[9])
    for cp in [ld_hid, ld_enc, ld_slot, ld_wq, ld_k, ld_v, ld_wo[2], ld_wo[1], ld_wo[3], ld_wo[0]]:
        cp.start()

    ld_hid.wait()
    wide_hid = hid_v[...].astype(jnp.float32)
    mean_square = jnp.mean(wide_hid * wide_hid, axis=-1, keepdims=True)
    normed = (wide_hid * lax.rsqrt(mean_square + 1e-06)).astype(jnp.bfloat16)
    norm_own[0] = normed[:, :half]
    norm_own[1] = normed[:, half:]

    ld_enc.wait()
    ld_slot.wait()
    slot_req = []
    for i in range(ROWS):
        mine = (w * DEPTH + d) * ROWS + i
        req = jnp.int32(0)
        for j in range(WIDE * ROWS):
            cand = (j // ROWS * DEPTH + d) * ROWS + j % ROWS
            req = jnp.where(cache_slot[cand] == mine, cand, req)
        slot_req.append(req)

    def sent_a():
        wait_bytes(norm_got, send_sem.at[0])

    def sent_q():
        wait_bytes(q_own.at[pl.ds(0, WIDE - 1)], send_sem.at[1])

    def sent_o():
        wait_bytes(q_oth, send_sem.at[2])

    pl.semaphore_wait(barrier, len(peers))
    for e in range(C):
        send(norm_own.at[1 - d], norm_got.at[c], 0, peer(wide_at((0, 0, e)), z, 1 - d))
    for o in range(1, NARROW):
        pl.semaphore_signal(in_sem, inc=1, device_id=peer(w, (z + o) % NARROW, d), device_id_type=MESH)

    ld_wq.wait()
    q_own[w] = jnp.dot(norm_own[d], wq_v[...], preferred_element_type=jnp.float32)
    for s in HOPS:
        send(q_own.at[w], q_own.at[w], 1, peer(wide_at(s), z, d))

    wait_bytes(norm_got, recv_sem.at[0])
    both = jnp.concatenate([norm_got[e].astype(jnp.float32) for e in range(C)], axis=0).astype(jnp.bfloat16)
    part = jnp.dot(
        both, wq_v[:, pl.ds(pl.multiple_of(c * cols, cols), cols)], preferred_element_type=jnp.float32
    )
    for e in range(C):
        q_out[e] = part[e * ROWS : (e + 1) * ROWS]
    for s in STEPS:
        send(q_out, q_oth.at[c, pl.ds(w // C * C, C)], 2, peer(wide_at(s), z, 1 - d))

    ld_k.wait()
    ld_v.wait()
    wait_bytes(q_own.at[pl.ds(0, WIDE - 1)], recv_sem.at[1])
    wait_bytes(q_oth, recv_sem.at[2])
    head_of = lax.broadcasted_iota(jnp.int32, (heads, feats), 1) // HDIM
    own_head = head_of == lax.broadcasted_iota(jnp.int32, (heads, feats), 0)
    row_id = lax.broadcasted_iota(jnp.int32, (ROWS, feats), 0)
    scores = []
    for i in range(ROWS):
        req = slot_req[i]
        src = req // (DEPTH * ROWS)
        other = jnp.concatenate([q_oth[e, src] for e in range(C)], axis=1)
        pair = (q_own[src] + other).astype(jnp.bfloat16).astype(jnp.float32)
        query = jnp.sum(jnp.where(row_id == req % ROWS, pair, 0.0), axis=0, keepdims=True)
        spread = jnp.where(own_head, query, 0.0).astype(jnp.bfloat16)
        score = lax.dot_general(
            spread, k_v[i], (((1,), (1,)), ((), ())), preferred_element_type=jnp.float32
        )
        position = lax.broadcasted_iota(jnp.int32, score.shape, 1)
        scores.append(jnp.where(position < enc_blocks[req] * BLOCK, score, -1e30))
    scores = jnp.concatenate(scores, axis=0)
    raised = jnp.exp(scores - jnp.max(scores, axis=-1, keepdims=True))
    shares = (raised / jnp.sum(raised, axis=-1, keepdims=True)).astype(jnp.bfloat16)
    for i in range(ROWS):
        ctx = jnp.dot(shares[i * heads : (i + 1) * heads], v_v[i], preferred_element_type=jnp.float32)
        ctx_v[pl.ds(i, 1), :] = jnp.sum(jnp.where(own_head, ctx, 0.0), axis=0, keepdims=True)
    ctx_b = ctx_v[...].astype(jnp.bfloat16)
    for dz in (2, 1, 3, 0):
        ld_wo[dz].wait()
        block = jnp.dot(ctx_b, wo_v[dz], preferred_element_type=jnp.float32).astype(jnp.bfloat16)
        fin_out[dz] = block
        if dz == 0:
            fin_all[w] = block
        if dz == 2:
            pl.semaphore_wait(in_sem, NARROW - 1)
        for s in HOPS if dz == 0 else STEPS:
            send(fin_out.at[dz], fin_all.at[dz * WIDE + w], 3, peer(wide_at(s), (z + dz) % NARROW, d))
    wait_bytes(fin_all.at[pl.ds(0, NARROW * WIDE - 1)], recv_sem.at[3])
    rows = []
    for i in range(ROWS):
        slot = cache_slot[(w * DEPTH + d) * ROWS + i]
        src = slot // (DEPTH * ROWS)
        pair = fin_all[src].astype(jnp.float32)
        for dz in range(1, NARROW):
            pair = pair + fin_all[dz * WIDE + src].astype(jnp.float32)
        rows.append(jnp.sum(jnp.where(row_id == slot % ROWS, pair, 0.0), axis=0, keepdims=True))
    out[...] = jnp.concatenate(rows, axis=0).astype(jnp.bfloat16)

    sent_a()
    sent_q()
    sent_o()
    wait_bytes(fin_all.at[pl.ds(0, NARROW * WIDE - 1)], send_sem.at[3])


def shards(hidden_state, query_weight, output_weight, cache_keys, cache_values, enc_blocks, cache_slot):
    rows, width = hidden_state.shape
    half, feats = query_weight.shape
    bf16, f32 = jnp.bfloat16, jnp.float32
    dma = pltpu.SemaphoreType.DMA
    operands = [
        pltpu.with_memory_space_constraint(a, pltpu.HBM)
        for a in (hidden_state, query_weight, output_weight, cache_keys, cache_values, enc_blocks, cache_slot)
    ]
    return pl.pallas_call(
        kernel,
        out_shape=jax.ShapeDtypeStruct((rows, feats), bf16),
        in_specs=[pl.BlockSpec(memory_space=pltpu.HBM)] * 7,
        out_specs=pl.BlockSpec(memory_space=pltpu.VMEM),
        scratch_shapes=[
            pltpu.VMEM((rows, width), bf16),
            pltpu.VMEM((half, feats), bf16),
            pltpu.VMEM((NARROW, feats, feats), bf16),
            pltpu.VMEM(cache_keys.shape, bf16),
            pltpu.VMEM(cache_values.shape, bf16),
            pltpu.SMEM(enc_blocks.shape, jnp.int32),
            pltpu.SMEM(cache_slot.shape, jnp.int32),
            pltpu.VMEM((2, rows, half), bf16),
            pltpu.VMEM((C, rows, half), bf16),
            pltpu.VMEM((WIDE, rows, feats), f32),
            pltpu.VMEM((C, rows, feats // C), f32),
            pltpu.VMEM((C, WIDE, rows, feats // C), f32),
            pltpu.VMEM((rows, feats), f32),
            pltpu.VMEM((NARROW, rows, feats), bf16),
            pltpu.VMEM((NARROW * WIDE, rows, feats), bf16),
            pltpu.SemaphoreType.REGULAR,
            dma((10,)), dma((4,)), dma((4,)),
        ],
        compiler_params=pltpu.CompilerParams(
            collective_id=0, has_side_effects=True, vmem_limit_bytes=48 * 1024 * 1024
        ),
    )(*operands)


def solution(mesh):
    placed = (
        P(("wide", "depth"), None),
        P("depth", "narrow"),
        P("narrow", None),
        P(("wide", "depth"), None, "narrow"),
        P(("wide", "depth"), None, "narrow"),
        P(),
        P(),
    )
    return jax.shard_map(
        shards,
        mesh=mesh,
        in_specs=placed,
        out_specs=P(("wide", "depth"), "narrow"),
        check_vma=False,
    )
```

```python
import jax
import jax.numpy as jnp
from jax import lax
from jax.experimental import pallas as pl
from jax.experimental.pallas import tpu as pltpu
from jax.sharding import PartitionSpec as P

HDIM = 64
BLOCK = 128
XH, Y, C = 2, 4, 2
WIDE, NARROW, DEPTH = 16, 4, 2
ROWS = 2
MESH = pl.DeviceIdType.MESH
STEPS = [(a, b, e) for a in (1, 0) for b in (2, 1, 3, 0) for e in (1, 0)]
HOPS = STEPS[:-1]


def kernel(
    hid, wq, wo, keys, vals, enc_hbm, slot_hbm, out,
    hid_v, wq_v, wo_v, k_v, v_v, enc_blocks, cache_slot,
    norm_own, norm_got, q_own, q_out, q_oth, ctx_v, fin_out, fin_all,
    in_sem, ld_sem, send_sem, recv_sem,
):
    w = lax.axis_index("wide")
    z = lax.axis_index("narrow")
    d = lax.axis_index("depth")
    xh, y, c = w // 8, (w // 2) % 4, w % 2
    half = wq.shape[0]
    feats = wq.shape[1]
    heads = feats // HDIM

    def wide_at(step):
        return (xh + step[0]) % XH * 8 + (y + step[1]) % Y * 2 + (c + step[2]) % C

    def peer(w_, z_, d_):
        return {"wide": w_, "narrow": z_, "depth": d_}

    def send(src, dst, which, to):
        cp = pltpu.make_async_remote_copy(
            src_ref=src, dst_ref=dst, send_sem=send_sem.at[which], recv_sem=recv_sem.at[which],
            device_id=to, device_id_type=MESH,
        )
        cp.start()

    def wait_bytes(ref, sem):
        pltpu.make_async_copy(ref, ref, sem).wait()

    barrier = pltpu.get_barrier_semaphore()
    peers = [peer(wide_at(s), z, d) for s in HOPS]
    peers += [peer(wide_at(s), z, 1 - d) for s in STEPS]
    peers += [peer(w, (z + o) % NARROW, d) for o in (2, 1, 3)]
    for p in peers:
        pl.semaphore_signal(barrier, inc=1, device_id=p, device_id_type=MESH)

    ld_hid = pltpu.make_async_copy(hid, hid_v, ld_sem.at[0])
    ld_wq = pltpu.make_async_copy(wq, wq_v, ld_sem.at[1])
    ld_k = pltpu.make_async_copy(keys, k_v, ld_sem.at[2])
    ld_v = pltpu.make_async_copy(vals, v_v, ld_sem.at[3])
    ld_wo = [
        pltpu.make_async_copy(
            wo.at[:, pl.ds(dz * feats, feats)], wo_v.at[dz], ld_sem.at[4 + dz]
        )
        for dz in range(4)
    ]
    ld_enc = pltpu.make_async_copy(enc_hbm, enc_blocks, ld_sem.at[8])
    ld_slot = pltpu.make_async_copy(slot_hbm, cache_slot, ld_sem.at[9])
    for cp in [ld_hid, ld_enc, ld_slot, ld_wq, ld_k, ld_v, *ld_wo]:
        cp.start()

    ld_hid.wait()
    wide_hid = hid_v[...].astype(jnp.float32)
    mean_square = jnp.mean(wide_hid * wide_hid, axis=-1, keepdims=True)
    normed = (wide_hid * lax.rsqrt(mean_square + 1e-06)).astype(jnp.bfloat16)
    norm_own[0] = normed[:, :half]
    norm_own[1] = normed[:, half:]

    ld_enc.wait()
    ld_slot.wait()
    slot_req = []
    for i in range(ROWS):
        mine = (w * DEPTH + d) * ROWS + i
        req = jnp.int32(0)
        for j in range(WIDE * ROWS):
            cand = (j // ROWS * DEPTH + d) * ROWS + j % ROWS
            req = jnp.where(cache_slot[cand] == mine, cand, req)
        slot_req.append(req)

    def sent_a():
        wait_bytes(norm_got, send_sem.at[0])

    def sent_q():
        wait_bytes(q_own.at[pl.ds(0, WIDE - 1)], send_sem.at[1])

    def sent_o():
        wait_bytes(q_oth, send_sem.at[2])

    pl.semaphore_wait(barrier, len(peers))
    send(norm_own.at[1 - d], norm_got, 0, peer(w, z, 1 - d))
    for o in range(1, NARROW):
        pl.semaphore_signal(in_sem, inc=1, device_id=peer(w, (z + o) % NARROW, d), device_id_type=MESH)

    ld_wq.wait()
    q_own[w] = jnp.dot(norm_own[d], wq_v[...], preferred_element_type=jnp.float32)
    for s in HOPS:
        send(q_own.at[w], q_own.at[w], 1, peer(wide_at(s), z, d))

    wait_bytes(norm_got, recv_sem.at[0])
    q_out[...] = jnp.dot(norm_got[...], wq_v[...], preferred_element_type=jnp.float32)
    for s in STEPS:
        send(q_out, q_oth.at[w], 2, peer(wide_at(s), z, 1 - d))

    ld_k.wait()
    ld_v.wait()
    wait_bytes(q_own.at[pl.ds(0, WIDE - 1)], recv_sem.at[1])
    wait_bytes(q_oth, recv_sem.at[2])
    head_of = lax.broadcasted_iota(jnp.int32, (heads, feats), 1) // HDIM
    own_head = head_of == lax.broadcasted_iota(jnp.int32, (heads, feats), 0)
    row_id = lax.broadcasted_iota(jnp.int32, (ROWS, feats), 0)
    scores = []
    for i in range(ROWS):
        req = slot_req[i]
        src = req // (DEPTH * ROWS)
        pair = (q_own[src] + q_oth[src]).astype(jnp.bfloat16).astype(jnp.float32)
        query = jnp.sum(jnp.where(row_id == req % ROWS, pair, 0.0), axis=0, keepdims=True)
        spread = jnp.where(own_head, query, 0.0).astype(jnp.bfloat16)
        score = lax.dot_general(
            spread, k_v[i], (((1,), (1,)), ((), ())), preferred_element_type=jnp.float32
        )
        position = lax.broadcasted_iota(jnp.int32, score.shape, 1)
        scores.append(jnp.where(position < enc_blocks[req] * BLOCK, score, -1e30))
    scores = jnp.concatenate(scores, axis=0)
    raised = jnp.exp(scores - jnp.max(scores, axis=-1, keepdims=True))
    shares = (raised / jnp.sum(raised, axis=-1, keepdims=True)).astype(jnp.bfloat16)
    for i in range(ROWS):
        ctx = jnp.dot(shares[i * heads : (i + 1) * heads], v_v[i], preferred_element_type=jnp.float32)
        ctx_v[pl.ds(i, 1), :] = jnp.sum(jnp.where(own_head, ctx, 0.0), axis=0, keepdims=True)
    ctx_b = ctx_v[...].astype(jnp.bfloat16)
    here = z * WIDE + w
    for to_z in range(NARROW):
        ld_wo[to_z].wait()
        block = jnp.dot(ctx_b, wo_v[to_z], preferred_element_type=jnp.float32).astype(jnp.bfloat16)
        fin_out[to_z] = block
        if to_z == 0:
            pl.semaphore_wait(in_sem, NARROW - 1)
        for s in HOPS:
            send(fin_out.at[to_z], fin_all.at[here], 3, peer(wide_at(s), to_z, d))

        @pl.when(z != to_z)
        def _():
            send(fin_out.at[to_z], fin_all.at[here], 3, peer(w, to_z, d))

    fin_all[here] = fin_out[z]
    wait_bytes(fin_all.at[pl.ds(0, NARROW * WIDE - 1)], recv_sem.at[3])
    rows = []
    for i in range(ROWS):
        slot = cache_slot[(w * DEPTH + d) * ROWS + i]
        src = slot // (DEPTH * ROWS)
        pair = fin_all[src].astype(jnp.float32)
        for from_z in range(1, NARROW):
            pair = pair + fin_all[from_z * WIDE + src].astype(jnp.float32)
        rows.append(jnp.sum(jnp.where(row_id == slot % ROWS, pair, 0.0), axis=0, keepdims=True))
    out[...] = jnp.concatenate(rows, axis=0).astype(jnp.bfloat16)

    sent_a()
    sent_q()
    sent_o()
    wait_bytes(fin_all.at[pl.ds(0, NARROW * WIDE - 1)], send_sem.at[3])


def shards(hidden_state, query_weight, output_weight, cache_keys, cache_values, enc_blocks, cache_slot):
    rows, width = hidden_state.shape
    half, feats = query_weight.shape
    bf16, f32 = jnp.bfloat16, jnp.float32
    dma = pltpu.SemaphoreType.DMA
    operands = [
        pltpu.with_memory_space_constraint(a, pltpu.HBM)
        for a in (hidden_state, query_weight, output_weight, cache_keys, cache_values, enc_blocks, cache_slot)
    ]
    return pl.pallas_call(
        kernel,
        out_shape=jax.ShapeDtypeStruct((rows, feats), bf16),
        in_specs=[pl.BlockSpec(memory_space=pltpu.HBM)] * 7,
        out_specs=pl.BlockSpec(memory_space=pltpu.VMEM),
        scratch_shapes=[
            pltpu.VMEM((rows, width), bf16),
            pltpu.VMEM((half, feats), bf16),
            pltpu.VMEM((NARROW, feats, feats), bf16),
            pltpu.VMEM(cache_keys.shape, bf16),
            pltpu.VMEM(cache_values.shape, bf16),
            pltpu.SMEM(enc_blocks.shape, jnp.int32),
            pltpu.SMEM(cache_slot.shape, jnp.int32),
            pltpu.VMEM((2, rows, half), bf16),
            pltpu.VMEM((rows, half), bf16),
            pltpu.VMEM((WIDE, rows, feats), f32),
            pltpu.VMEM((rows, feats), f32),
            pltpu.VMEM((WIDE, rows, feats), f32),
            pltpu.VMEM((rows, feats), f32),
            pltpu.VMEM((NARROW, rows, feats), bf16),
            pltpu.VMEM((NARROW * WIDE, rows, feats), bf16),
            pltpu.SemaphoreType.REGULAR,
            dma((10,)), dma((4,)), dma((4,)),
        ],
        compiler_params=pltpu.CompilerParams(
            collective_id=0, has_side_effects=True, vmem_limit_bytes=48 * 1024 * 1024
        ),
    )(*operands)


def solution(mesh):
    placed = (
        P(("wide", "depth"), None),
        P("depth", "narrow"),
        P("narrow", None),
        P(("wide", "depth"), None, "narrow"),
        P(("wide", "depth"), None, "narrow"),
        P(),
        P(),
    )
    return jax.shard_map(
        shards,
        mesh=mesh,
        in_specs=placed,
        out_specs=P(("wide", "depth"), "narrow"),
        check_vma=False,
    )
```

```python
import jax
import jax.numpy as jnp
from jax import lax
from jax.experimental import pallas as pl
from jax.experimental.pallas import tpu as pltpu
from jax.sharding import PartitionSpec as P

HDIM = 64
BLOCK = 128
XH, Y, C = 2, 4, 2
WIDE, NARROW, DEPTH = 16, 4, 2
ROWS = 2
MESH = pl.DeviceIdType.MESH
STEPS = [(a, b, e) for a in (1, 0) for b in (2, 1, 3, 0) for e in (1, 0)]
HOPS = STEPS[:-1]


def kernel(
    hid, wq, wo, keys, vals, enc_hbm, slot_hbm, out,
    hid_v, wq_v, wo_v, k_v, v_v, enc_blocks, cache_slot,
    norm_own, norm_got, q_own, q_out, q_oth, ctx_v, fin_out, fin_all,
    in_sem, ld_sem, send_sem, recv_sem,
):
    w = lax.axis_index("wide")
    z = lax.axis_index("narrow")
    d = lax.axis_index("depth")
    xh, y, c = w // 8, (w // 2) % 4, w % 2
    half = wq.shape[0]
    feats = wq.shape[1]
    heads = feats // HDIM

    def wide_at(step):
        return (xh + step[0]) % XH * 8 + (y + step[1]) % Y * 2 + (c + step[2]) % C

    def peer(w_, z_, d_):
        return {"wide": w_, "narrow": z_, "depth": d_}

    def send(src, dst, which, to):
        cp = pltpu.make_async_remote_copy(
            src_ref=src, dst_ref=dst, send_sem=send_sem.at[which], recv_sem=recv_sem.at[which],
            device_id=to, device_id_type=MESH,
        )
        cp.start()

    def wait_bytes(ref, sem):
        pltpu.make_async_copy(ref, ref, sem).wait()

    ld_hid = pltpu.make_async_copy(hid, hid_v, ld_sem.at[0])
    ld_wq = pltpu.make_async_copy(wq, wq_v, ld_sem.at[1])
    ld_k = pltpu.make_async_copy(keys, k_v, ld_sem.at[2])
    ld_v = pltpu.make_async_copy(vals, v_v, ld_sem.at[3])
    ld_wo = [
        pltpu.make_async_copy(
            wo.at[:, pl.ds(dz * feats, feats)], wo_v.at[dz], ld_sem.at[4 + dz]
        )
        for dz in range(4)
    ]
    ld_enc = pltpu.make_async_copy(enc_hbm, enc_blocks, ld_sem.at[8])
    ld_slot = pltpu.make_async_copy(slot_hbm, cache_slot, ld_sem.at[9])
    for cp in [ld_hid, ld_enc, ld_slot, ld_wq]:
        cp.start()

    barrier = pltpu.get_barrier_semaphore()
    peers = [peer(wide_at(s), z, d) for s in HOPS]
    peers += [peer(wide_at(s), z, 1 - d) for s in STEPS]
    peers += [peer(w, (z + o) % NARROW, d) for o in (2, 1, 3)]
    for p in peers:
        pl.semaphore_signal(barrier, inc=1, device_id=p, device_id_type=MESH)

    ld_hid.wait()
    wide_hid = hid_v[...].astype(jnp.float32)
    mean_square = jnp.mean(wide_hid * wide_hid, axis=-1, keepdims=True)
    normed = (wide_hid * lax.rsqrt(mean_square + 1e-06)).astype(jnp.bfloat16)
    norm_own[0] = normed[:, :half]
    norm_own[1] = normed[:, half:]

    ld_enc.wait()
    ld_slot.wait()
    slot_req = []
    for i in range(ROWS):
        mine = (w * DEPTH + d) * ROWS + i
        req = jnp.int32(0)
        for j in range(WIDE * ROWS):
            cand = (j // ROWS * DEPTH + d) * ROWS + j % ROWS
            req = jnp.where(cache_slot[cand] == mine, cand, req)
        slot_req.append(req)

    def sent_a():
        wait_bytes(norm_got, send_sem.at[0])

    def sent_q():
        wait_bytes(q_own.at[pl.ds(0, WIDE - 1)], send_sem.at[1])

    def sent_o():
        wait_bytes(q_oth, send_sem.at[2])

    pl.semaphore_wait(barrier, len(peers))
    send(norm_own.at[1 - d], norm_got, 0, peer(w, z, 1 - d))
    for o in range(1, NARROW):
        pl.semaphore_signal(in_sem, inc=1, device_id=peer(w, (z + o) % NARROW, d), device_id_type=MESH)

    ld_wq.wait()
    for cp in [ld_k, ld_v, *ld_wo]:
        cp.start()
    q_own[w] = jnp.dot(norm_own[d], wq_v[...], preferred_element_type=jnp.float32)
    for s in HOPS:
        send(q_own.at[w], q_own.at[w], 1, peer(wide_at(s), z, d))

    wait_bytes(norm_got, recv_sem.at[0])
    q_out[...] = jnp.dot(norm_got[...], wq_v[...], preferred_element_type=jnp.float32)
    for s in STEPS:
        send(q_out, q_oth.at[w], 2, peer(wide_at(s), z, 1 - d))

    ld_k.wait()
    ld_v.wait()
    wait_bytes(q_own.at[pl.ds(0, WIDE - 1)], recv_sem.at[1])
    wait_bytes(q_oth, recv_sem.at[2])
    head_of = lax.broadcasted_iota(jnp.int32, (heads, feats), 1) // HDIM
    own_head = head_of == lax.broadcasted_iota(jnp.int32, (heads, feats), 0)
    row_id = lax.broadcasted_iota(jnp.int32, (ROWS, feats), 0)
    scores = []
    for i in range(ROWS):
        req = slot_req[i]
        src = req // (DEPTH * ROWS)
        pair = (q_own[src] + q_oth[src]).astype(jnp.bfloat16).astype(jnp.float32)
        query = jnp.sum(jnp.where(row_id == req % ROWS, pair, 0.0), axis=0, keepdims=True)
        spread = jnp.where(own_head, query, 0.0).astype(jnp.bfloat16)
        score = lax.dot_general(
            spread, k_v[i], (((1,), (1,)), ((), ())), preferred_element_type=jnp.float32
        )
        position = lax.broadcasted_iota(jnp.int32, score.shape, 1)
        scores.append(jnp.where(position < enc_blocks[req] * BLOCK, score, -1e30))
    scores = jnp.concatenate(scores, axis=0)
    raised = jnp.exp(scores - jnp.max(scores, axis=-1, keepdims=True))
    shares = (raised / jnp.sum(raised, axis=-1, keepdims=True)).astype(jnp.bfloat16)
    for i in range(ROWS):
        ctx = jnp.dot(shares[i * heads : (i + 1) * heads], v_v[i], preferred_element_type=jnp.float32)
        ctx_v[pl.ds(i, 1), :] = jnp.sum(jnp.where(own_head, ctx, 0.0), axis=0, keepdims=True)
    ctx_b = ctx_v[...].astype(jnp.bfloat16)
    here = z * WIDE + w
    for to_z in range(NARROW):
        ld_wo[to_z].wait()
        block = jnp.dot(ctx_b, wo_v[to_z], preferred_element_type=jnp.float32).astype(jnp.bfloat16)
        fin_out[to_z] = block
        if to_z == 0:
            pl.semaphore_wait(in_sem, NARROW - 1)
        for s in HOPS:
            send(fin_out.at[to_z], fin_all.at[here], 3, peer(wide_at(s), to_z, d))

        @pl.when(z != to_z)
        def _():
            send(fin_out.at[to_z], fin_all.at[here], 3, peer(w, to_z, d))

    fin_all[here] = fin_out[z]
    wait_bytes(fin_all.at[pl.ds(0, NARROW * WIDE - 1)], recv_sem.at[3])
    rows = []
    for i in range(ROWS):
        slot = cache_slot[(w * DEPTH + d) * ROWS + i]
        src = slot // (DEPTH * ROWS)
        pair = fin_all[src].astype(jnp.float32)
        for from_z in range(1, NARROW):
            pair = pair + fin_all[from_z * WIDE + src].astype(jnp.float32)
        rows.append(jnp.sum(jnp.where(row_id == slot % ROWS, pair, 0.0), axis=0, keepdims=True))
    out[...] = jnp.concatenate(rows, axis=0).astype(jnp.bfloat16)

    sent_a()
    sent_q()
    sent_o()
    wait_bytes(fin_all.at[pl.ds(0, NARROW * WIDE - 1)], send_sem.at[3])


def shards(hidden_state, query_weight, output_weight, cache_keys, cache_values, enc_blocks, cache_slot):
    rows, width = hidden_state.shape
    half, feats = query_weight.shape
    bf16, f32 = jnp.bfloat16, jnp.float32
    dma = pltpu.SemaphoreType.DMA
    operands = [
        pltpu.with_memory_space_constraint(a, pltpu.HBM)
        for a in (hidden_state, query_weight, output_weight, cache_keys, cache_values, enc_blocks, cache_slot)
    ]
    return pl.pallas_call(
        kernel,
        out_shape=jax.ShapeDtypeStruct((rows, feats), bf16),
        in_specs=[pl.BlockSpec(memory_space=pltpu.HBM)] * 7,
        out_specs=pl.BlockSpec(memory_space=pltpu.VMEM),
        scratch_shapes=[
            pltpu.VMEM((rows, width), bf16),
            pltpu.VMEM((half, feats), bf16),
            pltpu.VMEM((NARROW, feats, feats), bf16),
            pltpu.VMEM(cache_keys.shape, bf16),
            pltpu.VMEM(cache_values.shape, bf16),
            pltpu.SMEM(enc_blocks.shape, jnp.int32),
            pltpu.SMEM(cache_slot.shape, jnp.int32),
            pltpu.VMEM((2, rows, half), bf16),
            pltpu.VMEM((rows, half), bf16),
            pltpu.VMEM((WIDE, rows, feats), f32),
            pltpu.VMEM((rows, feats), f32),
            pltpu.VMEM((WIDE, rows, feats), f32),
            pltpu.VMEM((rows, feats), f32),
            pltpu.VMEM((NARROW, rows, feats), bf16),
            pltpu.VMEM((NARROW * WIDE, rows, feats), bf16),
            pltpu.SemaphoreType.REGULAR,
            dma((10,)), dma((4,)), dma((4,)),
        ],
        compiler_params=pltpu.CompilerParams(
            collective_id=0, has_side_effects=True, vmem_limit_bytes=48 * 1024 * 1024
        ),
    )(*operands)


def solution(mesh):
    placed = (
        P(("wide", "depth"), None),
        P("depth", "narrow"),
        P("narrow", None),
        P(("wide", "depth"), None, "narrow"),
        P(("wide", "depth"), None, "narrow"),
        P(),
        P(),
    )
    return jax.shard_map(
        shards,
        mesh=mesh,
        in_specs=placed,
        out_specs=P(("wide", "depth"), "narrow"),
        check_vma=False,
    )
```

```python
import jax
import jax.numpy as jnp
from jax import lax
from jax.experimental import pallas as pl
from jax.experimental.pallas import tpu as pltpu
from jax.sharding import PartitionSpec as P

HDIM = 64
BLOCK = 128
XH, Y, C = 2, 4, 2
WIDE, NARROW, DEPTH = 16, 4, 2
ROWS = 2
MESH = pl.DeviceIdType.MESH
STEPS = [(a, b, e) for a in (1, 0) for b in (2, 1, 3, 0) for e in (1, 0)]
HOPS = STEPS[:-1]


def kernel(
    hid, wq, wo, keys, vals, enc_hbm, slot_hbm, out,
    hid_v, wq_v, wo_v, k_v, v_v, idx_s,
    norm_own, norm_got, q_own, q_out, q_oth, ctx_v, fin_out, fin_all,
    in_sem, ld_sem, send_sem, recv_sem,
):
    w = lax.axis_index("wide")
    z = lax.axis_index("narrow")
    d = lax.axis_index("depth")
    xh, y, c = w // 8, (w // 2) % 4, w % 2
    half = wq.shape[0]
    feats = wq.shape[1]
    heads = feats // HDIM

    def wide_at(step):
        return (xh + step[0]) % XH * 8 + (y + step[1]) % Y * 2 + (c + step[2]) % C

    def peer(w_, z_, d_):
        return {"wide": w_, "narrow": z_, "depth": d_}

    def send(src, dst, which, to):
        cp = pltpu.make_async_remote_copy(
            src_ref=src, dst_ref=dst, send_sem=send_sem.at[which], recv_sem=recv_sem.at[which],
            device_id=to, device_id_type=MESH,
        )
        cp.start()

    def wait_bytes(ref, sem):
        pltpu.make_async_copy(ref, ref, sem).wait()

    ld_hid = pltpu.make_async_copy(hid, hid_v, ld_sem.at[0])
    ld_wq = pltpu.make_async_copy(wq, wq_v, ld_sem.at[1])
    ld_k = pltpu.make_async_copy(keys, k_v, ld_sem.at[2])
    ld_v = pltpu.make_async_copy(vals, v_v, ld_sem.at[3])
    ld_wo = [
        pltpu.make_async_copy(
            wo.at[:, pl.ds(dz * feats, feats)], wo_v.at[dz], ld_sem.at[4]
        )
        for dz in range(4)
    ]
    ld_enc = pltpu.make_async_copy(enc_hbm, idx_s.at[0], ld_sem.at[5])
    ld_slot = pltpu.make_async_copy(slot_hbm, idx_s.at[1], ld_sem.at[5])
    for cp in [ld_hid, ld_enc, ld_slot, ld_wq]:
        cp.start()

    barrier = pltpu.get_barrier_semaphore()
    peers = [peer(wide_at(s), z, d) for s in HOPS]
    peers += [peer(wide_at(s), z, 1 - d) for s in STEPS]
    peers += [peer(w, (z + o) % NARROW, d) for o in (2, 1, 3)]
    for p in peers:
        pl.semaphore_signal(barrier, inc=1, device_id=p, device_id_type=MESH)

    ld_hid.wait()
    wide_hid = hid_v[...].astype(jnp.float32)
    mean_square = jnp.mean(wide_hid * wide_hid, axis=-1, keepdims=True)
    normed = (wide_hid * lax.rsqrt(mean_square + 1e-06)).astype(jnp.bfloat16)
    norm_own[0] = normed[:, :half]
    norm_own[1] = normed[:, half:]

    wait_bytes(idx_s, ld_sem.at[5])
    enc_blocks, cache_slot = idx_s.at[0], idx_s.at[1]
    slot_req = []
    for i in range(ROWS):
        mine = (w * DEPTH + d) * ROWS + i
        req = jnp.int32(0)
        for j in range(WIDE * ROWS):
            cand = (j // ROWS * DEPTH + d) * ROWS + j % ROWS
            req = jnp.where(cache_slot[cand] == mine, cand, req)
        slot_req.append(req)

    def sent_a():
        wait_bytes(norm_got, send_sem.at[0])

    def sent_q():
        wait_bytes(q_own.at[pl.ds(0, WIDE - 1)], send_sem.at[1])

    def sent_o():
        wait_bytes(q_oth, send_sem.at[2])

    pl.semaphore_wait(barrier, len(peers))
    send(norm_own.at[1 - d], norm_got, 0, peer(w, z, 1 - d))
    for o in range(1, NARROW):
        pl.semaphore_signal(in_sem, inc=1, device_id=peer(w, (z + o) % NARROW, d), device_id_type=MESH)

    ld_wq.wait()
    for cp in [ld_k, ld_v, *ld_wo]:
        cp.start()
    q_own[w] = jnp.dot(norm_own[d], wq_v[...], preferred_element_type=jnp.float32)
    for s in HOPS:
        send(q_own.at[w], q_own.at[w], 1, peer(wide_at(s), z, d))

    wait_bytes(norm_got, recv_sem.at[0])
    q_out[...] = jnp.dot(norm_got[...], wq_v[...], preferred_element_type=jnp.float32)
    for s in STEPS:
        send(q_out, q_oth.at[w], 2, peer(wide_at(s), z, 1 - d))

    ld_k.wait()
    ld_v.wait()
    wait_bytes(q_own.at[pl.ds(0, WIDE - 1)], recv_sem.at[1])
    wait_bytes(q_oth, recv_sem.at[2])
    head_of = lax.broadcasted_iota(jnp.int32, (heads, feats), 1) // HDIM
    own_head = head_of == lax.broadcasted_iota(jnp.int32, (heads, feats), 0)
    row_id = lax.broadcasted_iota(jnp.int32, (ROWS, feats), 0)
    scores = []
    for i in range(ROWS):
        req = slot_req[i]
        src = req // (DEPTH * ROWS)
        pair = (q_own[src] + q_oth[src]).astype(jnp.bfloat16).astype(jnp.float32)
        query = jnp.sum(jnp.where(row_id == req % ROWS, pair, 0.0), axis=0, keepdims=True)
        spread = jnp.where(own_head, query, 0.0).astype(jnp.bfloat16)
        score = lax.dot_general(
            spread, k_v[i], (((1,), (1,)), ((), ())), preferred_element_type=jnp.float32
        )
        position = lax.broadcasted_iota(jnp.int32, score.shape, 1)
        scores.append(jnp.where(position < enc_blocks[req] * BLOCK, score, -1e30))
    scores = jnp.concatenate(scores, axis=0)
    raised = jnp.exp(scores - jnp.max(scores, axis=-1, keepdims=True))
    shares = (raised / jnp.sum(raised, axis=-1, keepdims=True)).astype(jnp.bfloat16)
    for i in range(ROWS):
        ctx = jnp.dot(shares[i * heads : (i + 1) * heads], v_v[i], preferred_element_type=jnp.float32)
        ctx_v[pl.ds(i, 1), :] = jnp.sum(jnp.where(own_head, ctx, 0.0), axis=0, keepdims=True)
    ctx_b = ctx_v[...].astype(jnp.bfloat16)
    here = z * WIDE + w
    for to_z in range(NARROW):
        if to_z == 0:
            wait_bytes(wo_v, ld_sem.at[4])
        block = jnp.dot(ctx_b, wo_v[to_z], preferred_element_type=jnp.float32).astype(jnp.bfloat16)
        fin_out[to_z] = block
        if to_z == 0:
            pl.semaphore_wait(in_sem, NARROW - 1)
        for s in HOPS:
            send(fin_out.at[to_z], fin_all.at[here], 3, peer(wide_at(s), to_z, d))

        @pl.when(z != to_z)
        def _():
            send(fin_out.at[to_z], fin_all.at[here], 3, peer(w, to_z, d))

    fin_all[here] = fin_out[z]
    sent_a()
    sent_q()
    sent_o()
    wait_bytes(fin_all.at[pl.ds(0, NARROW * WIDE - 1)], recv_sem.at[3])
    rows = []
    for i in range(ROWS):
        slot = cache_slot[(w * DEPTH + d) * ROWS + i]
        src = slot // (DEPTH * ROWS)
        pair = fin_all[src].astype(jnp.float32)
        for from_z in range(1, NARROW):
            pair = pair + fin_all[from_z * WIDE + src].astype(jnp.float32)
        rows.append(jnp.sum(jnp.where(row_id == slot % ROWS, pair, 0.0), axis=0, keepdims=True))
    out[...] = jnp.concatenate(rows, axis=0).astype(jnp.bfloat16)

    wait_bytes(fin_all.at[pl.ds(0, NARROW * WIDE - 1)], send_sem.at[3])


def shards(hidden_state, query_weight, output_weight, cache_keys, cache_values, enc_blocks, cache_slot):
    rows, width = hidden_state.shape
    half, feats = query_weight.shape
    bf16, f32 = jnp.bfloat16, jnp.float32
    dma = pltpu.SemaphoreType.DMA
    operands = [
        pltpu.with_memory_space_constraint(a, pltpu.HBM)
        for a in (hidden_state, query_weight, output_weight, cache_keys, cache_values, enc_blocks, cache_slot)
    ]
    return pl.pallas_call(
        kernel,
        out_shape=jax.ShapeDtypeStruct((rows, feats), bf16),
        in_specs=[pl.BlockSpec(memory_space=pltpu.HBM)] * 7,
        out_specs=pl.BlockSpec(memory_space=pltpu.VMEM),
        scratch_shapes=[
            pltpu.VMEM((rows, width), bf16),
            pltpu.VMEM((half, feats), bf16),
            pltpu.VMEM((NARROW, feats, feats), bf16),
            pltpu.VMEM(cache_keys.shape, bf16),
            pltpu.VMEM(cache_values.shape, bf16),
            pltpu.SMEM((2, *enc_blocks.shape), jnp.int32),
            pltpu.VMEM((2, rows, half), bf16),
            pltpu.VMEM((rows, half), bf16),
            pltpu.VMEM((WIDE, rows, feats), f32),
            pltpu.VMEM((rows, feats), f32),
            pltpu.VMEM((WIDE, rows, feats), f32),
            pltpu.VMEM((rows, feats), f32),
            pltpu.VMEM((NARROW, rows, feats), bf16),
            pltpu.VMEM((NARROW * WIDE, rows, feats), bf16),
            pltpu.SemaphoreType.REGULAR,
            dma((6,)), dma((4,)), dma((4,)),
        ],
        compiler_params=pltpu.CompilerParams(
            collective_id=0, has_side_effects=True, vmem_limit_bytes=48 * 1024 * 1024
        ),
    )(*operands)


def solution(mesh):
    placed = (
        P(("wide", "depth"), None),
        P("depth", "narrow"),
        P("narrow", None),
        P(("wide", "depth"), None, "narrow"),
        P(("wide", "depth"), None, "narrow"),
        P(),
        P(),
    )
    return jax.shard_map(
        shards,
        mesh=mesh,
        in_specs=placed,
        out_specs=P(("wide", "depth"), "narrow"),
        check_vma=False,
    )
```

```python
import jax
import jax.numpy as jnp
from jax import lax
from jax.experimental import pallas as pl
from jax.experimental.pallas import tpu as pltpu
from jax.sharding import PartitionSpec as P

HDIM = 64
BLOCK = 128
XH, Y, C = 2, 4, 2
WIDE, NARROW, DEPTH = 16, 4, 2
ROWS = 2
MESH = pl.DeviceIdType.MESH
STEPS = [(a, b, e) for a in (1, 0) for b in (2, 1, 3, 0) for e in (1, 0)]
HOPS = STEPS[:-1]


def kernel(
    hid, wq, wo, keys, vals, enc_hbm, slot_hbm, out,
    hid_v, wq_v, wo_v, k_v, v_v, idx_s,
    norm_own, norm_got, q_own, q_out, q_oth, ctx_v, fin_out, fin_all,
    in_sem, ld_sem, send_sem, recv_sem,
):
    w = lax.axis_index("wide")
    z = lax.axis_index("narrow")
    d = lax.axis_index("depth")
    xh, y, c = w // 8, (w // 2) % 4, w % 2
    half = wq.shape[0]
    feats = wq.shape[1]
    heads = feats // HDIM

    def wide_at(step):
        return (xh + step[0]) % XH * 8 + (y + step[1]) % Y * 2 + (c + step[2]) % C

    def peer(w_, z_, d_):
        return {"wide": w_, "narrow": z_, "depth": d_}

    def send(src, dst, which, to):
        cp = pltpu.make_async_remote_copy(
            src_ref=src, dst_ref=dst, send_sem=send_sem.at[which], recv_sem=recv_sem.at[which],
            device_id=to, device_id_type=MESH,
        )
        cp.start()

    def wait_bytes(ref, sem):
        pltpu.make_async_copy(ref, ref, sem).wait()

    ld_hid = pltpu.make_async_copy(hid, hid_v, ld_sem.at[0])
    ld_wq = pltpu.make_async_copy(wq, wq_v, ld_sem.at[1])
    ld_k = pltpu.make_async_copy(keys, k_v, ld_sem.at[2])
    ld_v = pltpu.make_async_copy(vals, v_v, ld_sem.at[3])
    ld_wo = [
        pltpu.make_async_copy(
            wo.at[:, pl.ds(dz * feats, feats)], wo_v.at[dz], ld_sem.at[4]
        )
        for dz in range(4)
    ]
    ld_enc = pltpu.make_async_copy(enc_hbm, idx_s.at[0], ld_sem.at[5])
    ld_slot = pltpu.make_async_copy(slot_hbm, idx_s.at[1], ld_sem.at[5])
    for cp in [ld_hid, ld_enc, ld_slot, ld_wq]:
        cp.start()

    barrier = pltpu.get_barrier_semaphore()
    peers = [peer(wide_at(s), z, d) for s in HOPS]
    peers += [peer(wide_at(s), z, 1 - d) for s in STEPS]
    peers += [peer(w, (z + o) % NARROW, d) for o in (2, 1, 3)]
    for p in peers:
        pl.semaphore_signal(barrier, inc=1, device_id=p, device_id_type=MESH)

    ld_hid.wait()
    wide_hid = hid_v[...].astype(jnp.float32)
    mean_square = jnp.mean(wide_hid * wide_hid, axis=-1, keepdims=True)
    normed = (wide_hid * lax.rsqrt(mean_square + 1e-06)).astype(jnp.bfloat16)
    norm_own[0] = normed[:, :half]
    norm_own[1] = normed[:, half:]

    wait_bytes(idx_s, ld_sem.at[5])
    enc_blocks, cache_slot = idx_s.at[0], idx_s.at[1]
    slot_req = []
    for i in range(ROWS):
        mine = (w * DEPTH + d) * ROWS + i
        req = jnp.int32(0)
        for j in range(WIDE * ROWS):
            cand = (j // ROWS * DEPTH + d) * ROWS + j % ROWS
            req = jnp.where(cache_slot[cand] == mine, cand, req)
        slot_req.append(req)

    def sent_a():
        wait_bytes(norm_got, send_sem.at[0])

    def sent_q():
        wait_bytes(q_own.at[pl.ds(0, WIDE - 1)], send_sem.at[1])

    def sent_o():
        wait_bytes(q_oth, send_sem.at[2])

    pl.semaphore_wait(barrier, len(peers))
    send(norm_own.at[1 - d], norm_got, 0, peer(w, z, 1 - d))
    for o in range(1, NARROW):
        pl.semaphore_signal(in_sem, inc=1, device_id=peer(w, (z + o) % NARROW, d), device_id_type=MESH)

    ld_wq.wait()
    for cp in [ld_k, ld_v, *ld_wo]:
        cp.start()
    q_own[w] = jnp.dot(norm_own[d], wq_v[...], preferred_element_type=jnp.float32)
    for s in HOPS:
        send(q_own.at[w], q_own.at[w], 1, peer(wide_at(s), z, d))

    wait_bytes(norm_got, recv_sem.at[0])
    q_out[...] = jnp.dot(norm_got[...], wq_v[...], preferred_element_type=jnp.float32)
    for s in STEPS:
        send(q_out, q_oth.at[w], 2, peer(wide_at(s), z, 1 - d))

    ld_k.wait()
    ld_v.wait()
    wait_bytes(q_own.at[pl.ds(0, WIDE - 1)], recv_sem.at[1])
    wait_bytes(q_oth, recv_sem.at[2])
    head_of = lax.broadcasted_iota(jnp.int32, (heads, feats), 1) // HDIM
    own_head = head_of == lax.broadcasted_iota(jnp.int32, (heads, feats), 0)
    row_id = lax.broadcasted_iota(jnp.int32, (ROWS, feats), 0)
    scores = []
    for i in range(ROWS):
        req = slot_req[i]
        src = req // (DEPTH * ROWS)
        row = pl.ds(req % ROWS, 1)
        query = (q_own[src, row] + q_oth[src, row]).astype(jnp.bfloat16).astype(jnp.float32)
        spread = jnp.where(own_head, query, 0.0).astype(jnp.bfloat16)
        score = lax.dot_general(
            spread, k_v[i], (((1,), (1,)), ((), ())), preferred_element_type=jnp.float32
        )
        position = lax.broadcasted_iota(jnp.int32, score.shape, 1)
        scores.append(jnp.where(position < enc_blocks[req] * BLOCK, score, -1e30))
    scores = jnp.concatenate(scores, axis=0)
    raised = jnp.exp(scores - jnp.max(scores, axis=-1, keepdims=True))
    shares = (raised / jnp.sum(raised, axis=-1, keepdims=True)).astype(jnp.bfloat16)
    for i in range(ROWS):
        ctx = jnp.dot(shares[i * heads : (i + 1) * heads], v_v[i], preferred_element_type=jnp.float32)
        ctx_v[pl.ds(i, 1), :] = jnp.sum(jnp.where(own_head, ctx, 0.0), axis=0, keepdims=True)
    ctx_b = ctx_v[...].astype(jnp.bfloat16)
    here = z * WIDE + w
    for to_z in range(NARROW):
        if to_z == 0:
            wait_bytes(wo_v, ld_sem.at[4])
        block = jnp.dot(ctx_b, wo_v[to_z], preferred_element_type=jnp.float32).astype(jnp.bfloat16)
        fin_out[to_z] = block
        if to_z == 0:
            pl.semaphore_wait(in_sem, NARROW - 1)
        for s in HOPS:
            send(fin_out.at[to_z], fin_all.at[here], 3, peer(wide_at(s), to_z, d))

        @pl.when(z != to_z)
        def _():
            send(fin_out.at[to_z], fin_all.at[here], 3, peer(w, to_z, d))

    fin_all[here] = fin_out[z]
    sent_a()
    sent_q()
    sent_o()
    wait_bytes(fin_all.at[pl.ds(0, NARROW * WIDE - 1)], recv_sem.at[3])
    rows = []
    for i in range(ROWS):
        slot = cache_slot[(w * DEPTH + d) * ROWS + i]
        src = slot // (DEPTH * ROWS)
        pair = fin_all[src].astype(jnp.float32)
        for from_z in range(1, NARROW):
            pair = pair + fin_all[from_z * WIDE + src].astype(jnp.float32)
        rows.append(jnp.sum(jnp.where(row_id == slot % ROWS, pair, 0.0), axis=0, keepdims=True))
    out[...] = jnp.concatenate(rows, axis=0).astype(jnp.bfloat16)

    wait_bytes(fin_all.at[pl.ds(0, NARROW * WIDE - 1)], send_sem.at[3])


def shards(hidden_state, query_weight, output_weight, cache_keys, cache_values, enc_blocks, cache_slot):
    rows, width = hidden_state.shape
    half, feats = query_weight.shape
    bf16, f32 = jnp.bfloat16, jnp.float32
    dma = pltpu.SemaphoreType.DMA
    operands = [
        pltpu.with_memory_space_constraint(a, pltpu.HBM)
        for a in (hidden_state, query_weight, output_weight, cache_keys, cache_values, enc_blocks, cache_slot)
    ]
    return pl.pallas_call(
        kernel,
        out_shape=jax.ShapeDtypeStruct((rows, feats), bf16),
        in_specs=[pl.BlockSpec(memory_space=pltpu.HBM)] * 7,
        out_specs=pl.BlockSpec(memory_space=pltpu.VMEM),
        scratch_shapes=[
            pltpu.VMEM((rows, width), bf16),
            pltpu.VMEM((half, feats), bf16),
            pltpu.VMEM((NARROW, feats, feats), bf16),
            pltpu.VMEM(cache_keys.shape, bf16),
            pltpu.VMEM(cache_values.shape, bf16),
            pltpu.SMEM((2, *enc_blocks.shape), jnp.int32),
            pltpu.VMEM((2, rows, half), bf16),
            pltpu.VMEM((rows, half), bf16),
            pltpu.VMEM((WIDE, rows, feats), f32),
            pltpu.VMEM((rows, feats), f32),
            pltpu.VMEM((WIDE, rows, feats), f32),
            pltpu.VMEM((rows, feats), f32),
            pltpu.VMEM((NARROW, rows, feats), bf16),
            pltpu.VMEM((NARROW * WIDE, rows, feats), bf16),
            pltpu.SemaphoreType.REGULAR,
            dma((6,)), dma((4,)), dma((4,)),
        ],
        compiler_params=pltpu.CompilerParams(
            collective_id=0, has_side_effects=True, vmem_limit_bytes=48 * 1024 * 1024
        ),
    )(*operands)


def solution(mesh):
    placed = (
        P(("wide", "depth"), None),
        P("depth", "narrow"),
        P("narrow", None),
        P(("wide", "depth"), None, "narrow"),
        P(("wide", "depth"), None, "narrow"),
        P(),
        P(),
    )
    return jax.shard_map(
        shards,
        mesh=mesh,
        in_specs=placed,
        out_specs=P(("wide", "depth"), "narrow"),
        check_vma=False,
    )
```
